32 devices in a mesh: row: 4 (over y, core), col: 8 (over z, x).
Axes of the slice: x: 2, y: 2, z: 4, core: 2. Of those that a mesh axis runs over, the one named last changes fastest.
Arguments:
- rhs: float32 [8, 8192], P(None, ('row', 'col')), may hold values from -6 to 6
- stiff_diag: float32 [8192], P(('row', 'col')), may hold values from 1 to 4
- tiles: bfloat16 [4, 8, 8, 128, 128], P('row', 'col'), may hold values from -0.15625 to 0.15625
- tile_cols: int32 [4, 8, 8], P('row', 'col'), may hold values from 0 to 7
- tile_offsets: int32 [4, 8, 8], P('row', 'col'), may hold values from 0 to 1, as said below
- tile_counts: int32 [4, 8, 1], P('row', 'col'), may hold values from 4 to 8, as said below
Outputs:
- solution: float32 [8, 8192], P(None, ('row', 'col'))
- residual: float32 [8, 8192], P(None, ('row', 'col'))
The draws below stay inside these ranges and needn't reach their ends.
Inputs may be any that keep to these rules, and one draw needn't show every extreme that they name: `tile_offsets`: within one grid cell, slots t with the same t mod 8 carry different offsets. `tile_counts`: some grid cell has all 8 slots live.
All inputs are finite; a program needn't handle non-finite values.
Results may differ from the reference program's by a relative error of at most 0.0035.
Values may be sent and summed in bfloat16 or wider, within the bound.
No kernel may reach another device: no remote copies, remote signals or barrier semaphores. Data moves between devices by JAX's collectives and lax.ppermute only.
A program may use at most 64 MiB of HBM per device.

```python
import math
import jax
import jax.numpy as jnp
from jax import lax

BS = 128
PB = 2
SAMPLES = 8
STEPS = 3
SLOT = 1
TPD = 8
NB = 64
NDOF = 8192
N_ROW = 4
N_COL = 8


def draw_tile_offsets(key, part):
    scores = jax.random.randint(key, (N_ROW, N_COL, N_COL, PB), 0, 1 << 20) * PB + jnp.arange(PB, dtype=jnp.int32)
    order = jnp.argsort(scores, axis=-1)[..., :SLOT]
    return jnp.transpose(order, (0, 1, 3, 2)).reshape(N_ROW, N_COL, TPD).astype(jnp.int32)


def draw_tile_counts(key, part):
    cells = N_ROW * N_COL
    base = jax.random.randint(jax.random.fold_in(key, 11), (cells,), TPD // 2, TPD + 1)
    fullest = jax.random.randint(jax.random.fold_in(key, 12), (), 0, cells)
    base = jnp.where(jnp.arange(cells, dtype=jnp.int32) == fullest, TPD, base)
    return base.reshape(N_ROW, N_COL, 1).astype(jnp.int32)


def plant(drawn, rng, least, largest):
    shape = drawn.shape
    place = [jax.random.randint(jax.random.fold_in(rng, axis), (), 0, shape[axis]) for axis in range(len(shape))]
    drawn = drawn.at[tuple(place)].set(least)
    longest = shape.index(max(shape))
    place[longest] = (place[longest] + 1) % shape[longest]
    return drawn.at[tuple(place)].set(largest)


def levels(rng, extent, split, smallest, top_value):
    factor_of = 1.0
    for dim, blocks in split:
        draws = jax.random.uniform(jax.random.fold_in(jax.random.fold_in(rng, 6), dim), (blocks,), jnp.float32, smallest / len(split), top_value / len(split))
        factor_of = factor_of * jnp.repeat(jnp.exp(draws), extent[dim] // blocks).reshape((-1,) + (1,) * (len(extent) - 1 - dim))
    return factor_of


def bell_draw(rng, shape, deviation, bound, cuts=(), kind=jnp.bfloat16):
    entries = deviation * jax.random.normal(rng, shape, jnp.float32)
    if cuts:
        entries = entries * levels(rng, shape, cuts, -0.22, 0.18)
    return jnp.clip(entries, -bound, bound).astype(kind)


def setup_inputs(seed: int = 0) -> dict:
    seeds = jax.random.split(jax.random.key(seed), 7)
    return {
        "rhs": bell_draw(seeds[0], (SAMPLES, NDOF), 1.0, 6.0, ((1, 32),), jnp.float32),
        "stiff_diag": jnp.clip(jnp.exp(math.log(4.0) - 1.3862944 * jax.random.uniform(seeds[1], (NDOF,), jnp.float32) ** levels(seeds[1], (NDOF,), ((0, 32),), -0.2, 0.2)), 1.0, 4.0),
        "tiles": bell_draw(seeds[2], (N_ROW, N_COL, TPD, BS, BS), (BS * 12) ** -0.5, 0.15625, ((0, 4), (1, 8))),
        "tile_cols": plant(jax.random.randint(seeds[3], (N_ROW, N_COL, TPD), 0, PB * N_ROW), jax.random.fold_in(seeds[3], 1), 0, (PB * N_ROW) - 1).astype(jnp.int32),
        "tile_offsets": draw_tile_offsets(jax.random.fold_in(seeds[6], 71), 0),
        "tile_counts": draw_tile_counts(jax.random.fold_in(seeds[6], 71), 0),
    }


lower_bound = 0.3
upper_bound = 1.9


def apply_sparse(rounded, tiles, tile_cols, tile_offsets, tile_counts):
    blocks = rounded.astype(jnp.float32).reshape(SAMPLES, NB, BS)
    slot_ids = jnp.arange(TPD, dtype=jnp.int32)
    col_ids = jnp.arange(N_COL, dtype=jnp.int32)[:, None]

    def one_row(row_id):
        tile_row = tiles[row_id].astype(jnp.float32)
        cols = tile_cols[row_id]
        global_col = ((cols // PB) * N_COL + col_ids) * PB + cols % PB
        picked = blocks[:, global_col]
        prods = jnp.einsum("ctij,sctj->ctsi", tile_row, picked, precision=lax.Precision.HIGHEST)
        live = (slot_ids[None, :] < tile_counts[row_id][:, 0:1]).astype(jnp.float32)
        prods = prods * live[:, :, None, None]
        local_rows = (slot_ids[None, :] % N_COL) * PB + tile_offsets[row_id]
        return jax.ops.segment_sum(prods.reshape(N_COL * TPD, SAMPLES, BS), local_rows.reshape(-1), num_segments=PB * N_COL)

    gathered = lax.map(one_row, jnp.arange(N_ROW, dtype=jnp.int32))
    return jnp.transpose(gathered, (2, 0, 1, 3)).reshape(SAMPLES, NDOF)


def reference(rhs, stiff_diag, tiles, tile_cols, tile_offsets, tile_counts):
    theta = (upper_bound + lower_bound) / 2.0
    delta = (upper_bound - lower_bound) / 2.0
    sigma = theta / delta
    inverse = 1.0 / stiff_diag
    solution = jnp.zeros_like(rhs)
    residual = rhs
    rho = 1.0 / sigma
    direction = (1.0 / theta) * inverse[None, :] * residual
    for step in range(STEPS):
        solution = solution + direction
        rounded = direction.astype(jnp.bfloat16)
        image = stiff_diag[None, :] * direction + apply_sparse(rounded, tiles, tile_cols, tile_offsets, tile_counts)
        residual = residual - image
        if step + 1 < STEPS:
            rho_new = 1.0 / (2.0 * sigma - rho)
            direction = rho_new * rho * direction + (2.0 * rho_new / delta) * inverse[None, :] * residual
            rho = rho_new
    return (solution, residual)
```

```python
import functools

import jax
import jax.numpy as jnp
from jax import lax
from jax.experimental import pallas as pl
from jax.experimental.pallas import tpu as pltpu
from jax.sharding import PartitionSpec as P

STEPS = 3
VMEM_BYTES = 16 << 20

lower_bound = 0.3
upper_bound = 1.9

theta = (upper_bound + lower_bound) / 2.0
delta = (upper_bound - lower_bound) / 2.0
sigma = theta / delta


def coefficients():
    rho = 1.0 / sigma
    out = []
    for _ in range(STEPS - 1):
        rho_new = 1.0 / (2.0 * sigma - rho)
        out.append((rho_new * rho, 2.0 * rho_new / delta))
        rho = rho_new
    return out


def multiply(rounded, tiles, cols, count, out, rows, ncol, offsets=None):
    slots = tiles.shape[0]
    samples = rounded.shape[1]
    for t in range(slots):
        picked = rounded[cols[t]]
        prod = lax.dot_general(
            picked, tiles[t], (((1,), (1,)), ((), ())), preferred_element_type=jnp.float32
        )
        sent = jnp.where(t < count, prod, 0.0).astype(jnp.bfloat16)
        first = (t // ncol) * samples
        for r in range(rows):
            out[r * ncol + t % ncol, pl.ds(first, samples), :] = sent
            if offsets is not None:
                half = (slots // ncol) * samples
                out[r * ncol + t % ncol, pl.ds(half + first, samples), :] = jnp.full(
                    sent.shape, offsets[t], jnp.int32
                ).astype(jnp.float32).astype(jnp.bfloat16)


def part(packed, r, k, width):
    samples = packed.shape[1] - 1
    rhs = packed[r, :samples, k * width : (k + 1) * width]
    diag = packed[r, samples : samples + 1, k * width : (k + 1) * width]
    return rhs, diag


def coupled(moved, where, r, ncol, share, samples):
    def image(k):
        total = None
        for c in range(ncol):
            for a in range(share):
                piece = moved[r * ncol + c, pl.ds(a * samples, samples), :].astype(jnp.float32)
                off = where[r * ncol + c, pl.ds((share + a) * samples, samples), :]
                off = off.astype(jnp.float32)
                term = jnp.where(off == k, piece, 0.0)
                total = term if total is None else total + term
        return total

    return image


def first_kernel(dims, cols, offsets, count, packed, tiles, out, rounded):
    rows, ncol, piece, width = dims
    for r in range(rows):
        for k in range(piece):
            rhs, diag = part(packed, r, k, width)
            rounded[r * piece + k] = ((1.0 / theta) * (1.0 / diag) * rhs).astype(jnp.bfloat16)
    multiply(rounded, tiles, cols, count[0], out, rows, ncol, offsets)


def middle_kernel(dims, step, cols, count, packed, tiles, where, moved, *refs):
    rows, ncol, piece, width = dims
    samples = packed.shape[1] - 1
    share = tiles.shape[0] // ncol
    a, b = coefficients()[step]
    if step == 0:
        out, new_dir, new_res, new_sol, rounded = refs
    else:
        old_dir, old_res, old_sol, out, new_dir, new_res, new_sol, rounded = refs
    for r in range(rows):
        image = coupled(moved, where, r, ncol, share, samples)
        for k in range(piece):
            rhs, diag = part(packed, r, k, width)
            inverse = 1.0 / diag
            i = r * piece + k
            if step == 0:
                direction = (1.0 / theta) * inverse * rhs
                residual = rhs
                total = direction
            else:
                direction, residual, total = old_dir[i], old_res[i], old_sol[i]
            residual = residual - (diag * direction + image(k))
            direction = a * direction + b * inverse * residual
            new_dir[i] = direction
            new_res[i] = residual
            new_sol[i] = total + direction
            rounded[i] = direction.astype(jnp.bfloat16)
    multiply(rounded, tiles, cols, count[0], out, rows, ncol)


def last_kernel(dims, share, packed, where, moved, old_dir, old_res, old_sol, solution, residual):
    rows, ncol, piece, width = dims
    samples = packed.shape[1] - 1
    me = lax.axis_index("row")
    image = coupled(moved, where, me, ncol, share, samples)
    for k in range(piece):
        lanes = slice(k * width, (k + 1) * width)
        diag = packed[me, samples : samples + 1, lanes]
        i = me * piece + k
        solution[:, lanes] = old_sol[i]
        residual[:, lanes] = old_res[i] - (diag * old_dir[i] + image(k))


def body(rhs, stiff_diag, tiles, tile_cols, tile_offsets, tile_counts):
    tile_set = tiles[0, 0]
    cols = tile_cols[0, 0]
    offsets = tile_offsets[0, 0]
    count = tile_counts[0, 0]
    slots, width = tile_set.shape[:2]
    rows, ncol = lax.axis_size("row"), lax.axis_size("col")
    share = slots // ncol
    piece = stiff_diag.shape[0] // width
    samples = rhs.shape[0]
    blocks = rows * piece
    dims = (rows, ncol, piece, width)
    smem = pl.BlockSpec(memory_space=pltpu.SMEM)
    vmem = pl.BlockSpec(memory_space=pltpu.VMEM)
    state = jax.ShapeDtypeStruct((blocks, samples, width), jnp.float32)
    message = jax.ShapeDtypeStruct((rows * ncol, share * samples, width), jnp.bfloat16)
    wide = jax.ShapeDtypeStruct((rows * ncol, 2 * share * samples, width), jnp.bfloat16)
    scratch = [pltpu.VMEM((blocks, samples, width), jnp.bfloat16)]

    params = pltpu.CompilerParams(vmem_limit_bytes=VMEM_BYTES)

    def exchange(x):
        return lax.all_to_all(x, ("row", "col"), split_axis=0, concat_axis=0, tiled=True)

    packed = lax.all_gather(jnp.concatenate([rhs, stiff_diag[None, :]], axis=0), "row", axis=0)
    sent = pl.pallas_call(
        functools.partial(first_kernel, dims),
        out_shape=wide,
        in_specs=[smem] * 3 + [vmem] * 2,
        out_specs=vmem,
        scratch_shapes=scratch,
        compiler_params=params,
    )(cols, offsets, count, packed, tile_set)
    moved = exchange(sent)
    where = moved
    states = ()
    for step in range(STEPS - 1):
        sent, *states = pl.pallas_call(
            functools.partial(middle_kernel, dims, step),
            out_shape=(message, state, state, state),
            in_specs=[smem] * 2 + [vmem] * (4 + len(states)),
            out_specs=(vmem,) * 4,
            scratch_shapes=scratch,
            compiler_params=params,
        )(cols, count, packed, tile_set, where, moved, *states)
        moved = exchange(sent)
    out = jax.ShapeDtypeStruct(rhs.shape, jnp.float32)
    return pl.pallas_call(
        functools.partial(last_kernel, dims, share),
        out_shape=(out, out),
        in_specs=[vmem] * (3 + len(states)),
        out_specs=(vmem, vmem),
        compiler_params=params,
    )(packed, where, moved, *states)


def solution(mesh):
    in_specs = (
        P(None, ("row", "col")),
        P(("row", "col")),
        P("row", "col", None, None, None),
        P("row", "col", None),
        P("row", "col", None),
        P("row", "col", None),
    )
    out_specs = (P(None, ("row", "col")), P(None, ("row", "col")))
    return jax.shard_map(body, mesh=mesh, in_specs=in_specs, out_specs=out_specs, check_vma=False)
```

```python
import functools

import jax
import jax.numpy as jnp
from jax import lax
from jax.experimental import pallas as pl
from jax.experimental.pallas import tpu as pltpu
from jax.sharding import PartitionSpec as P

STEPS = 3
VMEM_BYTES = 16 << 20

lower_bound = 0.3
upper_bound = 1.9

theta = (upper_bound + lower_bound) / 2.0
delta = (upper_bound - lower_bound) / 2.0
sigma = theta / delta


def coefficients():
    rho = 1.0 / sigma
    out = []
    for _ in range(STEPS - 1):
        rho_new = 1.0 / (2.0 * sigma - rho)
        out.append((rho_new * rho, 2.0 * rho_new / delta))
        rho = rho_new
    return out


def prep_kernel(cols, offsets, count, rhs, diag, tiles, packed, held, column, offset, *scratch):
    line, cols_here, offsets_here, sems = scratch
    samples = rhs.shape[0]
    copies = [
        pltpu.make_async_copy(source, target, sems.at[i])
        for i, (source, target) in enumerate(
            [
                (cols, cols_here),
                (offsets, offsets_here),
                (diag, line),
                (rhs, packed.at[pl.ds(0, samples), :]),
                (tiles.at[0, 0], held),
            ]
        )
    ]
    for copy in copies:
        copy.start()
    for copy in copies[:3]:
        copy.wait()
    packed[samples : samples + 1, :] = line[...]
    for t in range(column.shape[0]):
        here = jnp.where(t < count[0, 0, 0], cols_here[0, 0, t], -1)
        column[t] = jnp.full(column.shape[1:], here, jnp.int32)
        offset[t] = jnp.full(offset.shape[1:], offsets_here[0, 0, t], jnp.int32)
    for copy in copies[3:]:
        copy.wait()


def multiply(directions, tiles, column, out, rows, ncol, offset=None):
    slots = tiles.shape[0]
    samples = column.shape[1]
    for t in range(slots):
        where = column[t]
        picked = jnp.zeros_like(directions[0])
        for j, direction in enumerate(directions):
            picked = jnp.where(where == j, direction, picked)
        sent = lax.dot_general(
            picked.astype(jnp.bfloat16),
            tiles[t],
            (((1,), (1,)), ((), ())),
            preferred_element_type=jnp.float32,
        ).astype(jnp.bfloat16)
        first = (t // ncol) * samples
        for r in range(rows):
            out[r * ncol + t % ncol, pl.ds(first, samples), :] = sent
            if offset is not None:
                half = (slots // ncol) * samples
                out[r * ncol + t % ncol, pl.ds(half + first, samples), :] = (
                    offset[t].astype(jnp.float32).astype(jnp.bfloat16)
                )


def part(packed, r, k, width):
    samples = packed.shape[1] - 1
    rhs = packed[r, :samples, k * width : (k + 1) * width]
    diag = packed[r, samples : samples + 1, k * width : (k + 1) * width]
    return rhs, diag


def coupled(moved, where, r, ncol, share, samples, piece):
    totals = [None] * piece
    for c in range(ncol):
        for a in range(share):
            term = moved[r * ncol + c, pl.ds(a * samples, samples), :].astype(jnp.float32)
            off = where[r * ncol + c, pl.ds((share + a) * samples, samples), :]
            off = off.astype(jnp.float32)
            for k in range(piece):
                mine = jnp.where(off == k, term, 0.0)
                totals[k] = mine if totals[k] is None else totals[k] + mine
    return totals


def first_kernel(dims, packed, tiles, column, offset, out):
    rows, ncol, piece, width = dims
    directions = []
    for r in range(rows):
        for k in range(piece):
            rhs, diag = part(packed, r, k, width)
            directions.append((1.0 / theta) * (1.0 / diag) * rhs)
    multiply(directions, tiles, column, out, rows, ncol, offset)


def middle_kernel(dims, step, packed, tiles, column, where, moved, *refs):
    rows, ncol, piece, width = dims
    samples = packed.shape[1] - 1
    share = tiles.shape[0] // ncol
    a, b = coefficients()[step]
    if step == 0:
        out, new_dir, new_res, new_sol = refs
    else:
        old_dir, old_res, old_sol, out, new_dir, new_res, new_sol = refs
    directions = []
    for r in range(rows):
        image = coupled(moved, where, r, ncol, share, samples, piece)
        for k in range(piece):
            rhs, diag = part(packed, r, k, width)
            inverse = 1.0 / diag
            i = r * piece + k
            if step == 0:
                direction = (1.0 / theta) * inverse * rhs
                residual = rhs
                total = direction
            else:
                direction, residual, total = old_dir[i], old_res[i], old_sol[i]
            residual = residual - (diag * direction + image[k])
            direction = a * direction + b * inverse * residual
            new_dir[i] = direction
            new_res[i] = residual
            new_sol[i] = total + direction
            directions.append(direction)
    multiply(directions, tiles, column, out, rows, ncol)


def last_kernel(dims, share, packed, where, moved, old_dir, old_res, old_sol, solution, residual):
    rows, ncol, piece, width = dims
    samples = packed.shape[1] - 1
    me = lax.axis_index("row")
    image = coupled(moved, where, me, ncol, share, samples, piece)
    for k in range(piece):
        lanes = slice(k * width, (k + 1) * width)
        diag = packed[me, samples : samples + 1, lanes]
        i = me * piece + k
        solution[:, lanes] = old_sol[i]
        residual[:, lanes] = old_res[i] - (diag * old_dir[i] + image[k])


def body(rhs, stiff_diag, tiles, tile_cols, tile_offsets, tile_counts):
    slots, width = tiles.shape[2:4]
    rows, ncol = lax.axis_size("row"), lax.axis_size("col")
    share = slots // ncol
    piece = stiff_diag.shape[0] // width
    samples = rhs.shape[0]
    blocks = rows * piece
    dims = (rows, ncol, piece, width)
    vmem = pl.BlockSpec(memory_space=pltpu.VMEM)
    hbm = pl.BlockSpec(memory_space=pltpu.HBM)
    state = jax.ShapeDtypeStruct((blocks, samples, width), jnp.float32)
    table = jax.ShapeDtypeStruct((slots, samples, width), jnp.int32)
    message = jax.ShapeDtypeStruct((rows * ncol, share * samples, width), jnp.bfloat16)
    wide = jax.ShapeDtypeStruct((rows * ncol, 2 * share * samples, width), jnp.bfloat16)
    params = pltpu.CompilerParams(vmem_limit_bytes=VMEM_BYTES)

    def exchange(x):
        return lax.all_to_all(x, ("row", "col"), split_axis=0, concat_axis=0, tiled=True)

    def far(x):
        return pltpu.with_memory_space_constraint(x, pltpu.HBM)

    packed, held, column, offset = pl.pallas_call(
        prep_kernel,
        out_shape=(
            jax.ShapeDtypeStruct((samples + 1, rhs.shape[1]), jnp.float32),
            jax.ShapeDtypeStruct(tiles.shape[2:], tiles.dtype),
            table,
            table,
        ),
        in_specs=[hbm] * 2 + [pl.BlockSpec(memory_space=pltpu.SMEM)] + [hbm] * 3,
        out_specs=(vmem,) * 4,
        scratch_shapes=[
            pltpu.VMEM((1, rhs.shape[1]), jnp.float32),
            pltpu.SMEM(tile_cols.shape, jnp.int32),
            pltpu.SMEM(tile_offsets.shape, jnp.int32),
            pltpu.SemaphoreType.DMA((5,)),
        ],
        compiler_params=params,
    )(far(tile_cols), far(tile_offsets), tile_counts, far(rhs), far(stiff_diag[None, :]), far(tiles))
    packed = lax.all_gather(packed, "row", axis=0)
    sent = pl.pallas_call(
        functools.partial(first_kernel, dims),
        out_shape=wide,
        in_specs=[vmem] * 4,
        out_specs=vmem,
        compiler_params=params,
    )(packed, held, column, offset)
    moved = where = exchange(sent)
    states = ()
    for step in range(STEPS - 1):
        sent, *states = pl.pallas_call(
            functools.partial(middle_kernel, dims, step),
            out_shape=(message, state, state, state),
            in_specs=[vmem] * (5 + len(states)),
            out_specs=(vmem,) * 4,
            compiler_params=params,
        )(packed, held, column, where, moved, *states)
        moved = exchange(sent)
    out = jax.ShapeDtypeStruct(rhs.shape, jnp.float32)
    return pl.pallas_call(
        functools.partial(last_kernel, dims, share),
        out_shape=(out, out),
        in_specs=[vmem] * (3 + len(states)),
        out_specs=(vmem, vmem),
        compiler_params=params,
    )(packed, where, moved, *states)


def solution(mesh):
    in_specs = (
        P(None, ("row", "col")),
        P(("row", "col")),
        P("row", "col", None, None, None),
        P("row", "col", None),
        P("row", "col", None),
        P("row", "col", None),
    )
    out_specs = (P(None, ("row", "col")), P(None, ("row", "col")))
    return jax.shard_map(body, mesh=mesh, in_specs=in_specs, out_specs=out_specs, check_vma=False)
```

```python
import functools

import jax
import jax.numpy as jnp
from jax import lax
from jax.experimental import pallas as pl
from jax.experimental.pallas import tpu as pltpu
from jax.sharding import PartitionSpec as P

STEPS = 3
VMEM_BYTES = 16 << 20
PAIR = 2

lower_bound = 0.3
upper_bound = 1.9

theta = (upper_bound + lower_bound) / 2.0
delta = (upper_bound - lower_bound) / 2.0
sigma = theta / delta


def coefficients():
    rho = 1.0 / sigma
    out = []
    for _ in range(STEPS - 1):
        rho_new = 1.0 / (2.0 * sigma - rho)
        out.append((rho_new * rho, 2.0 * rho_new / delta))
        rho = rho_new
    return out


def pack_kernel(rhs, diag, packed, line, sems):
    samples = rhs.shape[0]
    copies = [
        pltpu.make_async_copy(diag, line, sems.at[0]),
        pltpu.make_async_copy(rhs, packed.at[pl.ds(0, samples), :], sems.at[1]),
    ]
    for copy in copies:
        copy.start()
    copies[0].wait()
    packed[samples : samples + 1, :] = line[...]
    copies[1].wait()


def prep_kernel(piece, cols, offsets, count, tiles, held, column, offset, *scratch):
    cols_here, offsets_here, sems = scratch
    me = lax.axis_index("row")
    copies = [
        pltpu.make_async_copy(source, target, sems.at[i])
        for i, (source, target) in enumerate(
            [(cols, cols_here), (offsets, offsets_here), (tiles.at[0, 0], held)]
        )
    ]
    for copy in copies:
        copy.start()
    for copy in copies[:2]:
        copy.wait()
    for t in range(column.shape[0]):
        col = cols_here[0, 0, t]
        col = ((col // piece) ^ me) * piece + col % piece
        here = jnp.where(t < count[0, 0, 0], col, -1)
        column[t] = jnp.full(column.shape[1:], here, jnp.int32)
        offset[t] = jnp.full(offset.shape[1:], offsets_here[0, 0, t], jnp.int32)
    copies[2].wait()


def multiply(directions, tiles, column, out, rows, ncol, offset=None):
    slots = tiles.shape[0]
    samples = column.shape[1]
    for t in range(slots):
        where = column[t]
        picked = jnp.zeros_like(directions[0])
        for j, direction in enumerate(directions):
            picked = jnp.where(where == j, direction, picked)
        sent = lax.dot_general(
            picked.astype(jnp.bfloat16),
            tiles[t],
            (((1,), (1,)), ((), ())),
            preferred_element_type=jnp.float32,
        ).astype(jnp.bfloat16)
        first = (t // ncol) * samples
        for r in range(rows):
            place = r * ncol + t % ncol
            if offset is None:
                out[place, pl.ds(first, samples), :] = sent
            else:
                pairs = samples // PAIR
                first = (t // ncol) * (pairs + 1)
                out[place, pl.ds(first, pairs)] = sent.reshape(pairs, PAIR, sent.shape[1])
                out[place, first + pairs] = offset[t][:PAIR].astype(jnp.float32).astype(jnp.bfloat16)


def part(packed, k, width):
    samples = packed.shape[0] - 1
    rhs = packed[:samples, k * width : (k + 1) * width]
    diag = packed[samples : samples + 1, k * width : (k + 1) * width]
    return rhs, diag


def coupled(moved, where, r, ncol, share, samples, piece):
    totals = [None] * piece
    pairs = samples // PAIR
    for c in range(ncol):
        for a in range(share):
            place = r * ncol + c
            first = a * (pairs + 1)
            off = where[place, first + pairs].astype(jnp.float32)[:1]
            if moved is where:
                term = moved[place, pl.ds(first, pairs)].reshape(samples, off.shape[1])
            else:
                term = moved[place, pl.ds(a * samples, samples), :]
            term = term.astype(jnp.float32)
            for k in range(piece):
                mine = jnp.where(off == k, term, 0.0)
                totals[k] = mine if totals[k] is None else totals[k] + mine
    return totals


def first_kernel(dims, *refs):
    rows, ncol, piece, width = dims
    packed = refs[:rows]
    tiles, column, offset, out = refs[rows:]
    directions = []
    for p in range(rows):
        for k in range(piece):
            rhs, diag = part(packed[p], k, width)
            directions.append((1.0 / theta) * (1.0 / diag) * rhs)
    multiply(directions, tiles, column, out, rows, ncol, offset)


def middle_kernel(dims, step, *refs):
    rows, ncol, piece, width = dims
    packed = refs[:rows]
    tiles, column, where, moved = refs[rows : rows + 4]
    if step == 0:
        moved = where
    samples = packed[0].shape[0] - 1
    share = tiles.shape[0] // ncol
    a, b = coefficients()[step]
    if step == 0:
        out, new_dir, new_res, new_sol = refs[rows + 4 :]
    else:
        old_dir, old_res, old_sol, out, new_dir, new_res, new_sol = refs[rows + 4 :]
    me = lax.axis_index("row")
    directions = []
    for p in range(rows):
        image = coupled(moved, where, me ^ p, ncol, share, samples, piece)
        for k in range(piece):
            rhs, diag = part(packed[p], k, width)
            inverse = 1.0 / diag
            i = p * piece + k
            if step == 0:
                direction = (1.0 / theta) * inverse * rhs
                residual = rhs
                total = direction
            else:
                direction, residual, total = old_dir[i], old_res[i], old_sol[i]
            residual = residual - (diag * direction + image[k])
            direction = a * direction + b * inverse * residual
            new_dir[i] = direction
            new_res[i] = residual
            new_sol[i] = total + direction
            directions.append(direction)
    multiply(directions, tiles, column, out, rows, ncol)


def last_kernel(dims, share, packed, where, moved, old_dir, old_res, old_sol, solution, residual):
    rows, ncol, piece, width = dims
    samples = packed.shape[0] - 1
    me = lax.axis_index("row")
    image = coupled(moved, where, me, ncol, share, samples, piece)
    for k in range(piece):
        lanes = slice(k * width, (k + 1) * width)
        diag = packed[samples : samples + 1, lanes]
        solution[:, lanes] = old_sol[k]
        residual[:, lanes] = old_res[k] - (diag * old_dir[k] + image[k])


def body(rhs, stiff_diag, tiles, tile_cols, tile_offsets, tile_counts):
    slots, width = tiles.shape[2:4]
    rows, ncol = lax.axis_size("row"), lax.axis_size("col")
    share = slots // ncol
    piece = stiff_diag.shape[0] // width
    samples = rhs.shape[0]
    blocks = rows * piece
    dims = (rows, ncol, piece, width)
    vmem = pl.BlockSpec(memory_space=pltpu.VMEM)
    hbm = pl.BlockSpec(memory_space=pltpu.HBM)
    state = jax.ShapeDtypeStruct((blocks, samples, width), jnp.float32)
    table = jax.ShapeDtypeStruct((slots, samples, width), jnp.int32)
    message = jax.ShapeDtypeStruct((rows * ncol, share * samples, width), jnp.bfloat16)
    wide = jax.ShapeDtypeStruct(
        (rows * ncol, share * (samples // PAIR + 1), PAIR, width), jnp.bfloat16
    )
    params = pltpu.CompilerParams(vmem_limit_bytes=VMEM_BYTES)

    def exchange(x):
        return lax.all_to_all(x, ("row", "col"), split_axis=0, concat_axis=0, tiled=True)

    def far(x):
        return pltpu.with_memory_space_constraint(x, pltpu.HBM)

    packed = pl.pallas_call(
        pack_kernel,
        out_shape=jax.ShapeDtypeStruct((samples + 1, rhs.shape[1]), jnp.float32),
        in_specs=[hbm] * 2,
        out_specs=vmem,
        scratch_shapes=[
            pltpu.VMEM((1, rhs.shape[1]), jnp.float32),
            pltpu.SemaphoreType.DMA((2,)),
        ],
        compiler_params=params,
    )(far(rhs), far(stiff_diag[None, :]))
    held, column, offset = pl.pallas_call(
        functools.partial(prep_kernel, piece),
        out_shape=(jax.ShapeDtypeStruct(tiles.shape[2:], tiles.dtype), table, table),
        in_specs=[hbm] * 2 + [pl.BlockSpec(memory_space=pltpu.SMEM)] + [hbm],
        out_specs=(vmem,) * 3,
        scratch_shapes=[
            pltpu.SMEM(tile_cols.shape, jnp.int32),
            pltpu.SMEM(tile_offsets.shape, jnp.int32),
            pltpu.SemaphoreType.DMA((3,)),
        ],
        compiler_params=params,
        cost_estimate=pl.CostEstimate(flops=0, bytes_accessed=4 << 20, transcendentals=0),
    )(far(tile_cols), far(tile_offsets), tile_counts, far(tiles))

    pieces = {0: packed}
    bit = rows // 2
    while bit:
        swap = [(i, i ^ bit) for i in range(rows)]
        for p in sorted(pieces):
            pieces[p ^ bit] = lax.ppermute(pieces[p], "row", swap)
        if bit == rows // 2:
            pieces[bit], held, column, offset = lax.optimization_barrier(
                (pieces[bit], held, column, offset)
            )
        bit //= 2
    pieces = [pieces[p] for p in range(rows)]
    sent = pl.pallas_call(
        functools.partial(first_kernel, dims),
        out_shape=wide,
        in_specs=[vmem] * (rows + 3),
        out_specs=vmem,
        compiler_params=params,
    )(*pieces, held, column, offset)
    moved = where = exchange(sent)
    states = ()
    for step in range(STEPS - 1):
        sent, *states = pl.pallas_call(
            functools.partial(middle_kernel, dims, step),
            out_shape=(message, state, state, state),
            in_specs=[vmem] * (rows + 4 + len(states)),
            out_specs=(vmem,) * 4,
            compiler_params=params,
        )(*pieces, held, column, where, moved, *states)
        moved = exchange(sent)
    out = jax.ShapeDtypeStruct(rhs.shape, jnp.float32)
    return pl.pallas_call(
        functools.partial(last_kernel, dims, share),
        out_shape=(out, out),
        in_specs=[vmem] * (3 + len(states)),
        out_specs=(vmem, vmem),
        compiler_params=params,
    )(packed, where, moved, *states)


def solution(mesh):
    in_specs = (
        P(None, ("row", "col")),
        P(("row", "col")),
        P("row", "col", None, None, None),
        P("row", "col", None),
        P("row", "col", None),
        P("row", "col", None),
    )
    out_specs = (P(None, ("row", "col")), P(None, ("row", "col")))
    return jax.shard_map(body, mesh=mesh, in_specs=in_specs, out_specs=out_specs, check_vma=False)
```

```python
import functools

import jax
import jax.numpy as jnp
from jax import lax
from jax.experimental import pallas as pl
from jax.experimental.pallas import tpu as pltpu
from jax.sharding import PartitionSpec as P

STEPS = 3
VMEM_BYTES = 16 << 20
PAIR = 2

lower_bound = 0.3
upper_bound = 1.9

theta = (upper_bound + lower_bound) / 2.0
delta = (upper_bound - lower_bound) / 2.0
sigma = theta / delta


def coefficients():
    rho = 1.0 / sigma
    out = []
    for _ in range(STEPS - 1):
        rho_new = 1.0 / (2.0 * sigma - rho)
        out.append((rho_new * rho, 2.0 * rho_new / delta))
        rho = rho_new
    return out


def pack_kernel(rhs, diag, packed, line, sems):
    samples = rhs.shape[0]
    copies = [
        pltpu.make_async_copy(diag, line, sems.at[0]),
        pltpu.make_async_copy(rhs, packed.at[pl.ds(0, samples), :], sems.at[1]),
    ]
    for copy in copies:
        copy.start()
    copies[0].wait()
    packed[samples : samples + 1, :] = line[...]
    copies[1].wait()


def prep_kernel(piece, cols, offsets, count, tiles, held, column, offset, *scratch):
    cols_here, offsets_here, sems = scratch
    me = lax.axis_index("row")
    copies = [
        pltpu.make_async_copy(source, target, sems.at[i])
        for i, (source, target) in enumerate(
            [(cols, cols_here), (offsets, offsets_here), (tiles.at[0, 0], held)]
        )
    ]
    for copy in copies:
        copy.start()
    for copy in copies[:2]:
        copy.wait()
    for t in range(column.shape[0]):
        col = cols_here[0, 0, t]
        col = ((col // piece) ^ me) * piece + col % piece
        here = jnp.where(t < count[0, 0, 0], col, -1)
        column[t] = jnp.full(column.shape[1:], here, jnp.int32)
        offset[t] = jnp.full(offset.shape[1:], offsets_here[0, 0, t], jnp.int32)
    copies[2].wait()


def multiply(directions, tiles, column, out, rows, ncol, offset=None):
    slots = tiles.shape[0]
    samples = column.shape[1]
    for t in range(slots):
        where = column[t]
        picked = jnp.zeros_like(directions[0])
        for j, direction in enumerate(directions):
            picked = jnp.where(where == j, direction, picked)
        sent = lax.dot_general(
            picked.astype(jnp.bfloat16),
            tiles[t],
            (((1,), (1,)), ((), ())),
            preferred_element_type=jnp.float32,
        ).astype(jnp.bfloat16)
        first = (t // ncol) * samples
        for r in range(rows):
            place = r * ncol + t % ncol
            if offset is None:
                out[place, pl.ds(first, samples), :] = sent
            else:
                pairs = samples // PAIR
                first = (t // ncol) * (pairs + 1)
                out[place, pl.ds(first, pairs)] = sent.reshape(pairs, PAIR, sent.shape[1])
                out[place, first + pairs] = offset[t][:PAIR].astype(jnp.float32).astype(jnp.bfloat16)


def part(packed, k, width):
    samples = packed.shape[0] - 1
    rhs = packed[:samples, k * width : (k + 1) * width]
    diag = packed[samples : samples + 1, k * width : (k + 1) * width]
    return rhs, diag


def coupled(moved, where, r, ncol, share, samples, piece, base=None):
    totals = [None] * piece
    pairs = samples // PAIR
    for c in range(ncol):
        for a in range(share):
            place = r * ncol + c
            first = a * (pairs + 1)
            off = where[place, first + pairs].astype(jnp.float32)[:1]
            if moved is where:
                term = moved[place, pl.ds(first, pairs)].reshape(samples, off.shape[1])
            else:
                here = place if base is None else base + c
                term = moved[here, pl.ds(a * samples, samples), :]
            term = term.astype(jnp.float32)
            for k in range(piece):
                mine = jnp.where(off == k, term, 0.0)
                totals[k] = mine if totals[k] is None else totals[k] + mine
    return totals


def first_kernel(dims, *refs):
    rows, ncol, piece, width = dims
    packed = refs[:rows]
    tiles, column, offset, out = refs[rows:]
    directions = []
    for p in range(rows):
        for k in range(piece):
            rhs, diag = part(packed[p], k, width)
            directions.append((1.0 / theta) * (1.0 / diag) * rhs)
    multiply(directions, tiles, column, out, rows, ncol, offset)


def middle_kernel(dims, step, *refs):
    rows, ncol, piece, width = dims
    packed = refs[:rows]
    tiles, column, where, moved = refs[rows : rows + 4]
    if step == 0:
        moved = where
    samples = packed[0].shape[0] - 1
    share = tiles.shape[0] // ncol
    a, b = coefficients()[step]
    if step == 0:
        out, new_dir, new_res, new_sol = refs[rows + 4 :]
    else:
        old_dir, old_res, old_sol, out, new_dir, new_res, new_sol = refs[rows + 4 :]
    me = lax.axis_index("row")
    directions = []
    for p in range(rows):
        image = coupled(moved, where, me ^ p, ncol, share, samples, piece)
        for k in range(piece):
            rhs, diag = part(packed[p], k, width)
            inverse = 1.0 / diag
            i = p * piece + k
            if step == 0:
                direction = (1.0 / theta) * inverse * rhs
                residual = rhs
                total = direction
            else:
                direction, residual, total = old_dir[i], old_res[i], old_sol[i]
            residual = residual - (diag * direction + image[k])
            direction = a * direction + b * inverse * residual
            new_dir[i] = direction
            new_res[i] = residual
            new_sol[i] = total + direction
            directions.append(direction)
    multiply(directions, tiles, column, out, out.shape[0] // ncol, ncol)


def last_kernel(dims, share, packed, where, moved, old_dir, old_res, old_sol, solution, residual):
    rows, ncol, piece, width = dims
    samples = packed.shape[0] - 1
    me = lax.axis_index("row")
    image = coupled(moved, where, me, ncol, share, samples, piece, 0)
    for k in range(piece):
        lanes = slice(k * width, (k + 1) * width)
        diag = packed[samples : samples + 1, lanes]
        solution[:, lanes] = old_sol[k]
        residual[:, lanes] = old_res[k] - (diag * old_dir[k] + image[k])


def body(rhs, stiff_diag, tiles, tile_cols, tile_offsets, tile_counts):
    slots, width = tiles.shape[2:4]
    rows, ncol = lax.axis_size("row"), lax.axis_size("col")
    share = slots // ncol
    piece = stiff_diag.shape[0] // width
    samples = rhs.shape[0]
    blocks = rows * piece
    dims = (rows, ncol, piece, width)
    vmem = pl.BlockSpec(memory_space=pltpu.VMEM)
    hbm = pl.BlockSpec(memory_space=pltpu.HBM)
    state = jax.ShapeDtypeStruct((blocks, samples, width), jnp.float32)
    table = jax.ShapeDtypeStruct((slots, samples, width), jnp.int32)
    narrow = jax.ShapeDtypeStruct((ncol, share * samples, width), jnp.bfloat16)
    message = jax.ShapeDtypeStruct((rows * ncol, share * samples, width), jnp.bfloat16)
    wide = jax.ShapeDtypeStruct(
        (rows * ncol, share * (samples // PAIR + 1), PAIR, width), jnp.bfloat16
    )
    params = pltpu.CompilerParams(vmem_limit_bytes=VMEM_BYTES)

    def exchange(x, axes=("row", "col")):
        return lax.all_to_all(x, axes, split_axis=0, concat_axis=0, tiled=True)

    def far(x):
        return pltpu.with_memory_space_constraint(x, pltpu.HBM)

    packed = pl.pallas_call(
        pack_kernel,
        out_shape=jax.ShapeDtypeStruct((samples + 1, rhs.shape[1]), jnp.float32),
        in_specs=[hbm] * 2,
        out_specs=vmem,
        scratch_shapes=[
            pltpu.VMEM((1, rhs.shape[1]), jnp.float32),
            pltpu.SemaphoreType.DMA((2,)),
        ],
        compiler_params=params,
    )(far(rhs), far(stiff_diag[None, :]))
    held, column, offset = pl.pallas_call(
        functools.partial(prep_kernel, piece),
        out_shape=(jax.ShapeDtypeStruct(tiles.shape[2:], tiles.dtype), table, table),
        in_specs=[hbm] * 2 + [pl.BlockSpec(memory_space=pltpu.SMEM)] + [hbm],
        out_specs=(vmem,) * 3,
        scratch_shapes=[
            pltpu.SMEM(tile_cols.shape, jnp.int32),
            pltpu.SMEM(tile_offsets.shape, jnp.int32),
            pltpu.SemaphoreType.DMA((3,)),
        ],
        compiler_params=params,
        cost_estimate=pl.CostEstimate(flops=0, bytes_accessed=4 << 20, transcendentals=0),
    )(far(tile_cols), far(tile_offsets), tile_counts, far(tiles))

    pieces = {0: packed}
    for p in range(1, rows):
        pieces[p] = lax.ppermute(packed, "row", [(i, i ^ p) for i in range(rows)])
    pieces = [pieces[p] for p in range(rows)]
    sent = pl.pallas_call(
        functools.partial(first_kernel, dims),
        out_shape=wide,
        in_specs=[vmem] * (rows + 3),
        out_specs=vmem,
        compiler_params=params,
    )(*pieces, held, column, offset)
    moved = where = exchange(sent)
    states = ()
    for step in range(STEPS - 1):
        sent, *states = pl.pallas_call(
            functools.partial(middle_kernel, dims, step),
            out_shape=(message if step + 2 < STEPS else narrow, state, state, state),
            in_specs=[vmem] * (rows + 4 + len(states)),
            out_specs=(vmem,) * 4,
            compiler_params=params,
        )(*pieces, held, column, where, moved, *states)
        moved = exchange(sent, ("row", "col") if step + 2 < STEPS else "col")
    out = jax.ShapeDtypeStruct(rhs.shape, jnp.float32)
    return pl.pallas_call(
        functools.partial(last_kernel, dims, share),
        out_shape=(out, out),
        in_specs=[vmem] * (3 + len(states)),
        out_specs=(vmem, vmem),
        compiler_params=params,
    )(packed, where, moved, *states)


def solution(mesh):
    in_specs = (
        P(None, ("row", "col")),
        P(("row", "col")),
        P("row", "col", None, None, None),
        P("row", "col", None),
        P("row", "col", None),
        P("row", "col", None),
    )
    out_specs = (P(None, ("row", "col")), P(None, ("row", "col")))
    return jax.shard_map(body, mesh=mesh, in_specs=in_specs, out_specs=out_specs, check_vma=False)
```

```python
import functools

import jax
import jax.numpy as jnp
from jax import lax
from jax.experimental import pallas as pl
from jax.experimental.pallas import tpu as pltpu
from jax.sharding import PartitionSpec as P

STEPS = 3
VMEM_BYTES = 16 << 20
PAIR = 2

lower_bound = 0.3
upper_bound = 1.9

theta = (upper_bound + lower_bound) / 2.0
delta = (upper_bound - lower_bound) / 2.0
sigma = theta / delta


def coefficients():
    rho = 1.0 / sigma
    out = []
    for _ in range(STEPS - 1):
        rho_new = 1.0 / (2.0 * sigma - rho)
        out.append((rho_new * rho, 2.0 * rho_new / delta))
        rho = rho_new
    return out


def pack_kernel(rhs, diag, packed, line, sems):
    samples = rhs.shape[0]
    copies = [
        pltpu.make_async_copy(diag, line, sems.at[0]),
        pltpu.make_async_copy(rhs, packed.at[pl.ds(0, samples), :], sems.at[1]),
    ]
    for copy in copies:
        copy.start()
    copies[0].wait()
    packed[samples : samples + 1, :] = line[...]
    copies[1].wait()


def prep_kernel(piece, cols, offsets, count, tiles, held, column, offset, *scratch):
    cols_here, offsets_here, sems = scratch
    me = lax.axis_index("row")
    copies = [
        pltpu.make_async_copy(source, target, sems.at[i])
        for i, (source, target) in enumerate(
            [(cols, cols_here), (offsets, offsets_here), (tiles.at[0, 0], held)]
        )
    ]
    for copy in copies:
        copy.start()
    for copy in copies[:2]:
        copy.wait()
    for t in range(column.shape[0]):
        col = cols_here[0, 0, t]
        col = ((col // piece) ^ me) * piece + col % piece
        here = jnp.where(t < count[0, 0, 0], col, -1)
        column[t] = jnp.full(column.shape[1:], here, jnp.int32)
        offset[t] = jnp.full(offset.shape[1:], offsets_here[0, 0, t], jnp.int32)
    copies[2].wait()


def column_order(ncol):
    middle = ncol // 2 - 1
    return [middle] + [c for c in range(ncol) if c != middle]


def multiply(directions, tiles, column, out, rows, ncol, offset=None):
    slots = tiles.shape[0]
    samples = column.shape[1]
    for t in range(slots):
        where = column[t]
        picked = jnp.zeros_like(directions[0])
        for j, direction in enumerate(directions):
            picked = jnp.where(where == j, direction, picked)
        sent = lax.dot_general(
            picked.astype(jnp.bfloat16),
            tiles[t],
            (((1,), (1,)), ((), ())),
            preferred_element_type=jnp.float32,
        ).astype(jnp.bfloat16)
        first = (t // ncol) * samples
        for r in range(rows):
            place = r * ncol + t % ncol
            if rows == 1:
                place = column_order(ncol).index(t % ncol)
            if offset is None:
                out[place, pl.ds(first, samples), :] = sent
            else:
                pairs = samples // PAIR
                first = (t // ncol) * (pairs + 1)
                out[place, pl.ds(first, pairs)] = sent.reshape(pairs, PAIR, sent.shape[1])
                out[place, first + pairs] = offset[t][:PAIR].astype(jnp.float32).astype(jnp.bfloat16)


def part(packed, k, width):
    samples = packed.shape[0] - 1
    rhs = packed[:samples, k * width : (k + 1) * width]
    diag = packed[samples : samples + 1, k * width : (k + 1) * width]
    return rhs, diag


def coupled(moved, where, r, ncol, share, samples, piece, last=False):
    totals = [None] * piece
    pairs = samples // PAIR
    for c in range(ncol):
        for a in range(share):
            place = r * ncol + c
            first = a * (pairs + 1)
            off = where[place, first + pairs].astype(jnp.float32)[:1]
            if moved is where:
                term = moved[place, pl.ds(first, pairs)].reshape(samples, off.shape[1])
            else:
                here = place if not last else column_order(ncol).index(c)
                term = moved[here, pl.ds(a * samples, samples), :]
            term = term.astype(jnp.float32)
            for k in range(piece):
                mine = jnp.where(off == k, term, 0.0)
                totals[k] = mine if totals[k] is None else totals[k] + mine
    return totals


def first_kernel(dims, *refs):
    rows, ncol, piece, width = dims
    packed = refs[:rows]
    tiles, column, offset, out = refs[rows:]
    directions = []
    for p in range(rows):
        for k in range(piece):
            rhs, diag = part(packed[p], k, width)
            directions.append((1.0 / theta) * (1.0 / diag) * rhs)
    multiply(directions, tiles, column, out, rows, ncol, offset)


def middle_kernel(dims, step, *refs):
    rows, ncol, piece, width = dims
    packed = refs[:rows]
    tiles, column, where, moved = refs[rows : rows + 4]
    if step == 0:
        moved = where
    samples = packed[0].shape[0] - 1
    share = tiles.shape[0] // ncol
    a, b = coefficients()[step]
    if step == 0:
        out, new_dir, new_res, new_sol = refs[rows + 4 :]
    else:
        old_dir, old_res, old_sol, out, new_dir, new_res, new_sol = refs[rows + 4 :]
    me = lax.axis_index("row")
    directions = []
    for p in range(rows):
        image = coupled(moved, where, me ^ p, ncol, share, samples, piece)
        for k in range(piece):
            rhs, diag = part(packed[p], k, width)
            inverse = 1.0 / diag
            i = p * piece + k
            if step == 0:
                direction = (1.0 / theta) * inverse * rhs
                residual = rhs
                total = direction
            else:
                direction, residual, total = old_dir[i], old_res[i], old_sol[i]
            residual = residual - (diag * direction + image[k])
            direction = a * direction + b * inverse * residual
            new_dir[i] = direction
            new_res[i] = residual
            new_sol[i] = total + direction
            directions.append(direction)
    multiply(directions, tiles, column, out, out.shape[0] // ncol, ncol)


def last_kernel(dims, share, packed, where, moved, old_dir, old_res, old_sol, solution, residual):
    rows, ncol, piece, width = dims
    samples = packed.shape[0] - 1
    me = lax.axis_index("row")
    image = coupled(moved, where, me, ncol, share, samples, piece, True)
    for k in range(piece):
        lanes = slice(k * width, (k + 1) * width)
        diag = packed[samples : samples + 1, lanes]
        solution[:, lanes] = old_sol[k]
        residual[:, lanes] = old_res[k] - (diag * old_dir[k] + image[k])


def body(rhs, stiff_diag, tiles, tile_cols, tile_offsets, tile_counts):
    slots, width = tiles.shape[2:4]
    rows, ncol = lax.axis_size("row"), lax.axis_size("col")
    share = slots // ncol
    piece = stiff_diag.shape[0] // width
    samples = rhs.shape[0]
    blocks = rows * piece
    dims = (rows, ncol, piece, width)
    vmem = pl.BlockSpec(memory_space=pltpu.VMEM)
    hbm = pl.BlockSpec(memory_space=pltpu.HBM)
    state = jax.ShapeDtypeStruct((blocks, samples, width), jnp.float32)
    table = jax.ShapeDtypeStruct((slots, samples, width), jnp.int32)
    narrow = jax.ShapeDtypeStruct((ncol, share * samples, width), jnp.bfloat16)
    message = jax.ShapeDtypeStruct((rows * ncol, share * samples, width), jnp.bfloat16)
    wide = jax.ShapeDtypeStruct(
        (rows * ncol, share * (samples // PAIR + 1), PAIR, width), jnp.bfloat16
    )
    params = pltpu.CompilerParams(vmem_limit_bytes=VMEM_BYTES)

    def exchange(x):
        return lax.all_to_all(x, ("row", "col"), split_axis=0, concat_axis=0, tiled=True)

    def exchange_columns(x):
        return lax.all_to_all(
            x, "col", 0, 0, axis_index_groups=[column_order(ncol)], tiled=True
        )

    def far(x):
        return pltpu.with_memory_space_constraint(x, pltpu.HBM)

    packed = pl.pallas_call(
        pack_kernel,
        out_shape=jax.ShapeDtypeStruct((samples + 1, rhs.shape[1]), jnp.float32),
        in_specs=[hbm] * 2,
        out_specs=vmem,
        scratch_shapes=[
            pltpu.VMEM((1, rhs.shape[1]), jnp.float32),
            pltpu.SemaphoreType.DMA((2,)),
        ],
        compiler_params=params,
    )(far(rhs), far(stiff_diag[None, :]))
    held, column, offset = pl.pallas_call(
        functools.partial(prep_kernel, piece),
        out_shape=(jax.ShapeDtypeStruct(tiles.shape[2:], tiles.dtype), table, table),
        in_specs=[hbm] * 2 + [pl.BlockSpec(memory_space=pltpu.SMEM)] + [hbm],
        out_specs=(vmem,) * 3,
        scratch_shapes=[
            pltpu.SMEM(tile_cols.shape, jnp.int32),
            pltpu.SMEM(tile_offsets.shape, jnp.int32),
            pltpu.SemaphoreType.DMA((3,)),
        ],
        compiler_params=params,
        cost_estimate=pl.CostEstimate(flops=0, bytes_accessed=4 << 20, transcendentals=0),
    )(far(tile_cols), far(tile_offsets), tile_counts, far(tiles))

    pieces = {0: packed}
    for p in range(1, rows):
        pieces[p] = lax.ppermute(packed, "row", [(i, i ^ p) for i in range(rows)])
    pieces = [pieces[p] for p in range(rows)]
    sent = pl.pallas_call(
        functools.partial(first_kernel, dims),
        out_shape=wide,
        in_specs=[vmem] * (rows + 3),
        out_specs=vmem,
        compiler_params=params,
    )(*pieces, held, column, offset)
    moved = where = exchange(sent)
    states = ()
    for step in range(STEPS - 1):
        sent, *states = pl.pallas_call(
            functools.partial(middle_kernel, dims, step),
            out_shape=(message if step + 2 < STEPS else narrow, state, state, state),
            in_specs=[vmem] * (rows + 4 + len(states)),
            out_specs=(vmem,) * 4,
            compiler_params=params,
        )(*pieces, held, column, where, moved, *states)
        moved = exchange(sent) if step + 2 < STEPS else exchange_columns(sent)
    out = jax.ShapeDtypeStruct(rhs.shape, jnp.float32)
    return pl.pallas_call(
        functools.partial(last_kernel, dims, share),
        out_shape=(out, out),
        in_specs=[vmem] * (3 + len(states)),
        out_specs=(vmem, vmem),
        compiler_params=params,
    )(packed, where, moved, *states)


def solution(mesh):
    in_specs = (
        P(None, ("row", "col")),
        P(("row", "col")),
        P("row", "col", None, None, None),
        P("row", "col", None),
        P("row", "col", None),
        P("row", "col", None),
    )
    out_specs = (P(None, ("row", "col")), P(None, ("row", "col")))
    return jax.shard_map(body, mesh=mesh, in_specs=in_specs, out_specs=out_specs, check_vma=False)
```

```python
import functools

import jax
import jax.numpy as jnp
from jax import lax
from jax.experimental import pallas as pl
from jax.experimental.pallas import tpu as pltpu
from jax.sharding import PartitionSpec as P

STEPS = 3
VMEM_BYTES = 16 << 20
PAIR = 2
GROUP = 2

lower_bound = 0.3
upper_bound = 1.9

theta = (upper_bound + lower_bound) / 2.0
delta = (upper_bound - lower_bound) / 2.0
sigma = theta / delta


def coefficients():
    rho = 1.0 / sigma
    out = []
    for _ in range(STEPS - 1):
        rho_new = 1.0 / (2.0 * sigma - rho)
        out.append((rho_new * rho, 2.0 * rho_new / delta))
        rho = rho_new
    return out


def pack_kernel(rhs, diag, packed, line, sems):
    samples = rhs.shape[0]
    copies = [
        pltpu.make_async_copy(diag, line, sems.at[0]),
        pltpu.make_async_copy(rhs, packed.at[pl.ds(0, samples), :], sems.at[1]),
    ]
    for copy in copies:
        copy.start()
    copies[0].wait()
    packed[samples : samples + 1, :] = line[...]
    copies[1].wait()


def prep_kernel(piece, cols, offsets, count, tiles, held, column, offset, *scratch):
    cols_here, offsets_here, sems = scratch
    me = lax.axis_index("row")
    slots, width = tiles.shape[2:4]
    pairs = [(cols, cols_here), (offsets, offsets_here)]
    for t in range(slots):
        lanes = pl.ds(t % GROUP * width, width)
        pairs.append((tiles.at[0, 0, t], held.at[t // GROUP, :, lanes]))
    copies = [
        pltpu.make_async_copy(source, target, sems.at[i])
        for i, (source, target) in enumerate(pairs)
    ]
    for copy in copies:
        copy.start()
    for copy in copies[:2]:
        copy.wait()
    for t in range(column.shape[0]):
        col = cols_here[0, 0, t]
        col = ((col // piece) ^ me) * piece + col % piece
        here = jnp.where(t < count[0, 0, 0], col, -1)
        column[t] = jnp.full(column.shape[1:], here, jnp.int32)
        offset[t] = jnp.full(offset.shape[1:], offsets_here[0, 0, t], jnp.int32)
    for copy in copies[2:]:
        copy.wait()


def column_order(ncol):
    half = ncol // 2
    return list(range(half))[::-1] + list(range(half, ncol))[::-1]


def multiply(directions, tiles, column, out, rows, ncol, offset=None):
    slots, samples, width = column.shape
    order = column_order(ncol) if rows == 1 else list(range(ncol))
    blank = jnp.zeros((samples, width), jnp.bfloat16)
    for first in range(0, slots, GROUP):
        lines = []
        for g in range(GROUP):
            where = column[first + g]
            picked = jnp.zeros_like(directions[0])
            for j, direction in enumerate(directions):
                picked = jnp.where(where == j, direction, picked)
            picked = picked.astype(jnp.bfloat16)
            line = [picked if h == g else blank for h in range(GROUP)]
            lines.append(jnp.concatenate(line, axis=1))
        sent = lax.dot_general(
            jnp.concatenate(lines, axis=0),
            tiles[first // GROUP],
            (((1,), (1,)), ((), ())),
            preferred_element_type=jnp.float32,
        )
        for g in range(GROUP):
            t = first + g
            mine = sent[g * samples : (g + 1) * samples].astype(jnp.bfloat16)
            for r in range(rows):
                place = r * ncol + order.index(t % ncol)
                if offset is None:
                    out[place, pl.ds((t // ncol) * samples, samples), :] = mine
                else:
                    pairs = samples // PAIR
                    begin = (t // ncol) * (pairs + 1)
                    out[place, pl.ds(begin, pairs)] = mine.reshape(pairs, PAIR, width)
                    out[place, begin + pairs] = (
                        offset[t][:PAIR].astype(jnp.float32).astype(jnp.bfloat16)
                    )


def part(packed, k, width):
    samples = packed.shape[0] - 1
    rhs = packed[:samples, k * width : (k + 1) * width]
    diag = packed[samples : samples + 1, k * width : (k + 1) * width]
    return rhs, diag


def coupled(moved, where, r, ncol, share, samples, piece, kept=None, last=False):
    totals = [None] * piece
    pairs = samples // PAIR
    order = column_order(ncol)
    for c in range(ncol):
        for a in range(share):
            place = r * ncol + c
            if kept is not None:
                first = a * (pairs + 1)
                term = moved[place, pl.ds(first, pairs)].reshape(samples, moved.shape[3])
                off = moved[place, first + pairs].astype(jnp.float32)[:1]
                off = jnp.broadcast_to(off, term.shape)
                kept[place * share + a] = off
            else:
                here = order.index(c) if last else place
                term = moved[here, pl.ds(a * samples, samples), :]
                off = where[place * share + a]
            term = term.astype(jnp.float32)
            for k in range(piece):
                mine = jnp.where(off == k, term, 0.0)
                totals[k] = mine if totals[k] is None else totals[k] + mine
    return totals


def first_kernel(dims, *refs):
    rows, ncol, piece, width = dims
    packed = refs[:rows]
    tiles, column, offset, out = refs[rows:]
    directions = []
    for p in range(rows):
        for k in range(piece):
            rhs, diag = part(packed[p], k, width)
            directions.append((1.0 / theta) * (1.0 / diag) * rhs)
    multiply(directions, tiles, column, out, rows, ncol, offset)


def middle_kernel(dims, step, *refs):
    rows, ncol, piece, width = dims
    packed = refs[:rows]
    tiles, column, moved = refs[rows : rows + 3]
    samples = packed[0].shape[0] - 1
    share = column.shape[0] // ncol
    a, b = coefficients()[step]
    where = kept = None
    if step == 0:
        out, new_dir, new_res, new_sol, kept = refs[rows + 3 :]
    else:
        where, old_dir, old_res, old_sol, out, new_dir, new_res, new_sol = refs[rows + 3 :]
    me = lax.axis_index("row")
    directions = []
    for p in range(rows):
        image = coupled(moved, where, me ^ p, ncol, share, samples, piece, kept)
        for k in range(piece):
            rhs, diag = part(packed[p], k, width)
            inverse = 1.0 / diag
            i = p * piece + k
            if step == 0:
                direction = (1.0 / theta) * inverse * rhs
                residual = rhs
                total = direction
            else:
                direction, residual, total = old_dir[i], old_res[i], old_sol[i]
            residual = residual - (diag * direction + image[k])
            direction = a * direction + b * inverse * residual
            new_dir[i] = direction
            new_res[i] = residual
            new_sol[i] = total + direction
            directions.append(direction)
    multiply(directions, tiles, column, out, out.shape[0] // ncol, ncol)


def last_kernel(dims, share, packed, where, moved, old_dir, old_res, old_sol, solution, residual):
    rows, ncol, piece, width = dims
    samples = packed.shape[0] - 1
    me = lax.axis_index("row")
    image = coupled(moved, where, me, ncol, share, samples, piece, last=True)
    for k in range(piece):
        lanes = slice(k * width, (k + 1) * width)
        diag = packed[samples : samples + 1, lanes]
        solution[:, lanes] = old_sol[k]
        residual[:, lanes] = old_res[k] - (diag * old_dir[k] + image[k])


def body(rhs, stiff_diag, tiles, tile_cols, tile_offsets, tile_counts):
    slots, width = tiles.shape[2:4]
    rows, ncol = lax.axis_size("row"), lax.axis_size("col")
    share = slots // ncol
    piece = stiff_diag.shape[0] // width
    samples = rhs.shape[0]
    blocks = rows * piece
    dims = (rows, ncol, piece, width)
    vmem = pl.BlockSpec(memory_space=pltpu.VMEM)
    hbm = pl.BlockSpec(memory_space=pltpu.HBM)
    state = jax.ShapeDtypeStruct((blocks, samples, width), jnp.float32)
    grouped = jax.ShapeDtypeStruct((slots // GROUP, width, GROUP * width), tiles.dtype)
    kept = jax.ShapeDtypeStruct((rows * ncol * share, samples, width), jnp.float32)
    table = jax.ShapeDtypeStruct((slots, samples, width), jnp.int32)
    narrow = jax.ShapeDtypeStruct((ncol, share * samples, width), jnp.bfloat16)
    message = jax.ShapeDtypeStruct((rows * ncol, share * samples, width), jnp.bfloat16)
    wide = jax.ShapeDtypeStruct(
        (rows * ncol, share * (samples // PAIR + 1), PAIR, width), jnp.bfloat16
    )
    params = pltpu.CompilerParams(vmem_limit_bytes=VMEM_BYTES)

    def exchange(x):
        return lax.all_to_all(x, ("row", "col"), split_axis=0, concat_axis=0, tiled=True)

    def exchange_columns(x):
        return lax.all_to_all(
            x, "col", 0, 0, axis_index_groups=[column_order(ncol)], tiled=True
        )

    def far(x):
        return pltpu.with_memory_space_constraint(x, pltpu.HBM)

    packed = pl.pallas_call(
        pack_kernel,
        out_shape=jax.ShapeDtypeStruct((samples + 1, rhs.shape[1]), jnp.float32),
        in_specs=[hbm] * 2,
        out_specs=vmem,
        scratch_shapes=[
            pltpu.VMEM((1, rhs.shape[1]), jnp.float32),
            pltpu.SemaphoreType.DMA((2,)),
        ],
        compiler_params=params,
    )(far(rhs), far(stiff_diag[None, :]))
    held, column, offset = pl.pallas_call(
        functools.partial(prep_kernel, piece),
        out_shape=(grouped, table, table),
        in_specs=[hbm] * 2 + [pl.BlockSpec(memory_space=pltpu.SMEM)] + [hbm],
        out_specs=(vmem,) * 3,
        scratch_shapes=[
            pltpu.SMEM(tile_cols.shape, jnp.int32),
            pltpu.SMEM(tile_offsets.shape, jnp.int32),
            pltpu.SemaphoreType.DMA((slots + 2,)),
        ],
        compiler_params=params,
        cost_estimate=pl.CostEstimate(flops=0, bytes_accessed=4 << 20, transcendentals=0),
    )(far(tile_cols), far(tile_offsets), tile_counts, far(tiles))

    pieces = {0: packed}
    for p in range(1, rows):
        pieces[p] = lax.ppermute(packed, "row", [(i, i ^ p) for i in range(rows)])
    pieces = [pieces[p] for p in range(rows)]
    sent = pl.pallas_call(
        functools.partial(first_kernel, dims),
        out_shape=wide,
        in_specs=[vmem] * (rows + 3),
        out_specs=vmem,
        compiler_params=params,
    )(*pieces, held, column, offset)
    moved = exchange(sent)
    states = []
    for step in range(STEPS - 1):
        shapes = [message if step + 2 < STEPS else narrow, state, state, state]
        if step == 0:
            shapes.append(kept)
        results = pl.pallas_call(
            functools.partial(middle_kernel, dims, step),
            out_shape=shapes,
            in_specs=[vmem] * (rows + 3 + len(states)),
            out_specs=[vmem] * len(shapes),
            compiler_params=params,
        )(*pieces, held, column, moved, *states)
        sent = results[0]
        if step == 0:
            where = results[4]
        states = [where, *results[1:4]]
        moved = exchange(sent) if step + 2 < STEPS else exchange_columns(sent)
    out = jax.ShapeDtypeStruct(rhs.shape, jnp.float32)
    return pl.pallas_call(
        functools.partial(last_kernel, dims, share),
        out_shape=(out, out),
        in_specs=[vmem] * 6,
        out_specs=(vmem, vmem),
        compiler_params=params,
    )(packed, where, moved, *states[1:])


def solution(mesh):
    in_specs = (
        P(None, ("row", "col")),
        P(("row", "col")),
        P("row", "col", None, None, None),
        P("row", "col", None),
        P("row", "col", None),
        P("row", "col", None),
    )
    out_specs = (P(None, ("row", "col")), P(None, ("row", "col")))
    return jax.shard_map(body, mesh=mesh, in_specs=in_specs, out_specs=out_specs, check_vma=False)
```

```python
import functools
import math

import jax
import jax.numpy as jnp
from jax import lax
from jax.experimental import pallas as pl
from jax.experimental.pallas import tpu as pltpu
from jax.sharding import PartitionSpec as P

STEPS = 3
VMEM_BYTES = 16 << 20
PAIR = 2
GROUP = 2

lower_bound = 0.3
upper_bound = 1.9

theta = (upper_bound + lower_bound) / 2.0
delta = (upper_bound - lower_bound) / 2.0
sigma = theta / delta


def coefficients():
    rho = 1.0 / sigma
    out = []
    for _ in range(STEPS - 1):
        rho_new = 1.0 / (2.0 * sigma - rho)
        out.append((rho_new * rho, 2.0 * rho_new / delta))
        rho = rho_new
    return out


def pack_kernel(rhs, diag, packed, line, sems):
    samples = rhs.shape[0]
    copies = [
        pltpu.make_async_copy(diag, line, sems.at[0]),
        pltpu.make_async_copy(rhs, packed.at[pl.ds(0, samples), :], sems.at[1]),
    ]
    for copy in copies:
        copy.start()
    copies[0].wait()
    packed[samples : samples + 1, :] = line[...]
    copies[1].wait()


def prep_kernel(piece, cols, offsets, count, tiles, held, column, offset, *scratch):
    cols_here, offsets_here, sems = scratch
    me = lax.axis_index("row")
    slots, width = tiles.shape[2:4]
    pairs = [(cols, cols_here), (offsets, offsets_here)]
    for t in range(slots):
        lanes = pl.ds(t % GROUP * width, width)
        pairs.append((tiles.at[0, 0, t], held.at[t // GROUP, :, lanes]))
    copies = [
        pltpu.make_async_copy(source, target, sems.at[i])
        for i, (source, target) in enumerate(pairs)
    ]
    for copy in copies:
        copy.start()
    for copy in copies[:2]:
        copy.wait()
    for t in range(column.shape[0]):
        col = cols_here[0, 0, t]
        col = ((col // piece) ^ me) * piece + col % piece
        here = jnp.where(t < count[0, 0, 0], col, -1)
        column[t] = jnp.full(column.shape[1:], here, jnp.int32)
        offset[t] = jnp.full(offset.shape[1:], offsets_here[0, 0, t], jnp.int32)
    for copy in copies[2:]:
        copy.wait()


def stride(rows, ncol):
    n = rows * ncol
    return n - 13 if n > 13 and math.gcd(n, 13) == 1 else 1


def column_order(ncol):
    half = ncol // 2
    return list(range(half))[::-1] + list(range(half, ncol))[::-1]


def multiply(directions, tiles, column, out, rows, ncol, offset=None):
    slots, samples, width = column.shape
    order = column_order(ncol)
    blank = jnp.zeros((samples, width), jnp.bfloat16)
    for first in range(0, slots, GROUP):
        lines = []
        for g in range(GROUP):
            where = column[first + g]
            picked = jnp.zeros_like(directions[0])
            for j, direction in enumerate(directions):
                picked = jnp.where(where == j, direction, picked)
            picked = picked.astype(jnp.bfloat16)
            line = [picked if h == g else blank for h in range(GROUP)]
            lines.append(jnp.concatenate(line, axis=1))
        sent = lax.dot_general(
            jnp.concatenate(lines, axis=0),
            tiles[first // GROUP],
            (((1,), (1,)), ((), ())),
            preferred_element_type=jnp.float32,
        )
        for g in range(GROUP):
            t = first + g
            mine = sent[g * samples : (g + 1) * samples].astype(jnp.bfloat16)
            for r in range(rows):
                place = stride(rows, ncol) * (r * ncol + t % ncol) % (rows * ncol)
                if rows == 1:
                    place = order.index(t % ncol)
                if offset is None:
                    out[place, pl.ds((t // ncol) * samples, samples), :] = mine
                else:
                    pairs = samples // PAIR
                    begin = (t // ncol) * (pairs + 1)
                    out[place, pl.ds(begin, pairs)] = mine.reshape(pairs, PAIR, width)
                    out[place, begin + pairs] = (
                        offset[t][:PAIR].astype(jnp.float32).astype(jnp.bfloat16)
                    )


def part(packed, k, width):
    samples = packed.shape[0] - 1
    rhs = packed[:samples, k * width : (k + 1) * width]
    diag = packed[samples : samples + 1, k * width : (k + 1) * width]
    return rhs, diag


def coupled(moved, where, p, rows, ncol, share, samples, piece, kept=None):
    totals = [None] * piece
    pairs = samples // PAIR
    order = column_order(ncol)
    step = stride(rows, ncol)
    begin = step * (lax.axis_index("row") ^ p)
    for c in range(ncol):
        if moved.shape[0] == ncol:
            place = order.index(c)
        else:
            high, low = divmod(step * c % (rows * ncol), ncol)
            place = ((begin + high) & (rows - 1)) * ncol + low
        for a in range(share):
            keep = (p * ncol + c) * share + a
            if kept is not None:
                first = a * (pairs + 1)
                term = moved[place, pl.ds(first, pairs)].reshape(samples, moved.shape[3])
                off = moved[place, first + pairs].astype(jnp.float32)[:1]
                off = jnp.broadcast_to(off, term.shape)
                kept[keep] = off
            else:
                term = moved[place, pl.ds(a * samples, samples), :]
                off = where[keep]
            term = term.astype(jnp.float32)
            for k in range(piece):
                mine = jnp.where(off == k, term, 0.0)
                totals[k] = mine if totals[k] is None else totals[k] + mine
    return totals


def first_kernel(dims, *refs):
    rows, ncol, piece, width = dims
    packed = refs[:rows]
    tiles, column, offset, out = refs[rows:]
    directions = []
    for p in range(rows):
        for k in range(piece):
            rhs, diag = part(packed[p], k, width)
            directions.append((1.0 / theta) * (1.0 / diag) * rhs)
    multiply(directions, tiles, column, out, rows, ncol, offset)


def middle_kernel(dims, step, *refs):
    rows, ncol, piece, width = dims
    packed = refs[:rows]
    tiles, column, moved = refs[rows : rows + 3]
    samples = packed[0].shape[0] - 1
    share = column.shape[0] // ncol
    a, b = coefficients()[step]
    where = kept = None
    if step == 0:
        out, new_dir, new_res, new_sol, kept = refs[rows + 3 :]
    else:
        where, old_dir, old_res, old_sol, out, new_dir, new_res, new_sol = refs[rows + 3 :]
    directions = []
    for p in range(rows):
        image = coupled(moved, where, p, rows, ncol, share, samples, piece, kept)
        for k in range(piece):
            rhs, diag = part(packed[p], k, width)
            inverse = 1.0 / diag
            i = p * piece + k
            if step == 0:
                direction = (1.0 / theta) * inverse * rhs
                residual = rhs
                total = direction
            else:
                direction, residual, total = old_dir[i], old_res[i], old_sol[i]
            residual = residual - (diag * direction + image[k])
            direction = a * direction + b * inverse * residual
            new_dir[i] = direction
            new_res[i] = residual
            new_sol[i] = total + direction
            directions.append(direction)
    multiply(directions, tiles, column, out, out.shape[0] // ncol, ncol)


def last_kernel(dims, share, packed, where, moved, old_dir, old_res, old_sol, solution, residual):
    rows, ncol, piece, width = dims
    samples = packed.shape[0] - 1
    image = coupled(moved, where, 0, rows, ncol, share, samples, piece)
    for k in range(piece):
        lanes = slice(k * width, (k + 1) * width)
        diag = packed[samples : samples + 1, lanes]
        solution[:, lanes] = old_sol[k]
        residual[:, lanes] = old_res[k] - (diag * old_dir[k] + image[k])


def body(rhs, stiff_diag, tiles, tile_cols, tile_offsets, tile_counts):
    slots, width = tiles.shape[2:4]
    rows, ncol = lax.axis_size("row"), lax.axis_size("col")
    share = slots // ncol
    piece = stiff_diag.shape[0] // width
    samples = rhs.shape[0]
    blocks = rows * piece
    dims = (rows, ncol, piece, width)
    vmem = pl.BlockSpec(memory_space=pltpu.VMEM)
    hbm = pl.BlockSpec(memory_space=pltpu.HBM)
    state = jax.ShapeDtypeStruct((blocks, samples, width), jnp.float32)
    grouped = jax.ShapeDtypeStruct((slots // GROUP, width, GROUP * width), tiles.dtype)
    kept = jax.ShapeDtypeStruct((rows * ncol * share, samples, width), jnp.float32)
    table = jax.ShapeDtypeStruct((slots, samples, width), jnp.int32)
    narrow = jax.ShapeDtypeStruct((ncol, share * samples, width), jnp.bfloat16)
    message = jax.ShapeDtypeStruct((rows * ncol, share * samples, width), jnp.bfloat16)
    wide = jax.ShapeDtypeStruct(
        (rows * ncol, share * (samples // PAIR + 1), PAIR, width), jnp.bfloat16
    )
    params = pltpu.CompilerParams(vmem_limit_bytes=VMEM_BYTES)

    def exchange(x):
        everyone = [0] * (rows * ncol)
        for i in range(rows * ncol):
            everyone[stride(rows, ncol) * i % (rows * ncol)] = i
        return lax.all_to_all(
            x, ("row", "col"), 0, 0, axis_index_groups=[everyone], tiled=True
        )

    def exchange_columns(x):
        return lax.all_to_all(
            x, "col", 0, 0, axis_index_groups=[column_order(ncol)], tiled=True
        )

    def far(x):
        return pltpu.with_memory_space_constraint(x, pltpu.HBM)

    packed = pl.pallas_call(
        pack_kernel,
        out_shape=jax.ShapeDtypeStruct((samples + 1, rhs.shape[1]), jnp.float32),
        in_specs=[hbm] * 2,
        out_specs=vmem,
        scratch_shapes=[
            pltpu.VMEM((1, rhs.shape[1]), jnp.float32),
            pltpu.SemaphoreType.DMA((2,)),
        ],
        compiler_params=params,
    )(far(rhs), far(stiff_diag[None, :]))
    held, column, offset = pl.pallas_call(
        functools.partial(prep_kernel, piece),
        out_shape=(grouped, table, table),
        in_specs=[hbm] * 2 + [pl.BlockSpec(memory_space=pltpu.SMEM)] + [hbm],
        out_specs=(vmem,) * 3,
        scratch_shapes=[
            pltpu.SMEM(tile_cols.shape, jnp.int32),
            pltpu.SMEM(tile_offsets.shape, jnp.int32),
            pltpu.SemaphoreType.DMA((slots + 2,)),
        ],
        compiler_params=params,
        cost_estimate=pl.CostEstimate(flops=0, bytes_accessed=4 << 20, transcendentals=0),
    )(far(tile_cols), far(tile_offsets), tile_counts, far(tiles))

    pieces = {0: packed}
    for p in range(1, rows):
        pieces[p] = lax.ppermute(packed, "row", [(i, i ^ p) for i in range(rows)])
    pieces = [pieces[p] for p in range(rows)]
    sent = pl.pallas_call(
        functools.partial(first_kernel, dims),
        out_shape=wide,
        in_specs=[vmem] * (rows + 3),
        out_specs=vmem,
        compiler_params=params,
    )(*pieces, held, column, offset)
    moved = exchange(sent)
    states = []
    for step in range(STEPS - 1):
        shapes = [message if step + 2 < STEPS else narrow, state, state, state]
        if step == 0:
            shapes.append(kept)
        results = pl.pallas_call(
            functools.partial(middle_kernel, dims, step),
            out_shape=shapes,
            in_specs=[vmem] * (rows + 3 + len(states)),
            out_specs=[vmem] * len(shapes),
            compiler_params=params,
        )(*pieces, held, column, moved, *states)
        sent = results[0]
        if step == 0:
            where = results[4]
        states = [where, *results[1:4]]
        moved = exchange(sent) if step + 2 < STEPS else exchange_columns(sent)
    out = jax.ShapeDtypeStruct(rhs.shape, jnp.float32)
    return pl.pallas_call(
        functools.partial(last_kernel, dims, share),
        out_shape=(out, out),
        in_specs=[vmem] * 6,
        out_specs=(vmem, vmem),
        compiler_params=params,
    )(packed, where, moved, *states[1:])


def solution(mesh):
    in_specs = (
        P(None, ("row", "col")),
        P(("row", "col")),
        P("row", "col", None, None, None),
        P("row", "col", None),
        P("row", "col", None),
        P("row", "col", None),
    )
    out_specs = (P(None, ("row", "col")), P(None, ("row", "col")))
    return jax.shard_map(body, mesh=mesh, in_specs=in_specs, out_specs=out_specs, check_vma=False)
```

```python
import functools
import math

import jax
import jax.numpy as jnp
from jax import lax
from jax.experimental import pallas as pl
from jax.experimental.pallas import tpu as pltpu
from jax.sharding import PartitionSpec as P

STEPS = 3
VMEM_BYTES = 16 << 20
PAIR = 2
GROUP = 2

lower_bound = 0.3
upper_bound = 1.9

theta = (upper_bound + lower_bound) / 2.0
delta = (upper_bound - lower_bound) / 2.0
sigma = theta / delta


def coefficients():
    rho = 1.0 / sigma
    out = []
    for _ in range(STEPS - 1):
        rho_new = 1.0 / (2.0 * sigma - rho)
        out.append((rho_new * rho, 2.0 * rho_new / delta))
        rho = rho_new
    return out


def pack_kernel(rhs, diag, packed, line, sems):
    samples = rhs.shape[0]
    copies = [
        pltpu.make_async_copy(diag, line, sems.at[0]),
        pltpu.make_async_copy(rhs, packed.at[pl.ds(0, samples), :], sems.at[1]),
    ]
    for copy in copies:
        copy.start()
    copies[0].wait()
    packed[samples : samples + 1, :] = line[...]
    copies[1].wait()


def prep_kernel(piece, cols, offsets, count, tiles, held, column, offset, *scratch):
    cols_here, offsets_here, sems = scratch
    me = lax.axis_index("row")
    slots, width = tiles.shape[2:4]
    pairs = [(cols, cols_here), (offsets, offsets_here)]
    for t in range(slots):
        lanes = pl.ds(t % GROUP * width, width)
        pairs.append((tiles.at[0, 0, t], held.at[t // GROUP, :, lanes]))
    copies = [
        pltpu.make_async_copy(source, target, sems.at[i])
        for i, (source, target) in enumerate(pairs)
    ]
    for copy in copies:
        copy.start()
    for copy in copies[:2]:
        copy.wait()
    for t in range(column.shape[0]):
        col = cols_here[0, 0, t]
        col = ((col // piece) ^ me) * piece + col % piece
        here = jnp.where(t < count[0, 0, 0], col, -1)
        column[t] = jnp.full(column.shape[1:], here, jnp.int32)
        offset[t] = jnp.full(offset.shape[1:], offsets_here[0, 0, t], jnp.int32)
    for copy in copies[2:]:
        copy.wait()


def stride(rows, ncol, turn):
    n = rows * ncol
    less = (5, 13)[turn]
    return n - less if n > less and math.gcd(n, less) == 1 else 1


def column_order(ncol):
    half = ncol // 2
    return list(range(half))[::-1] + list(range(half, ncol))[::-1]


def multiply(directions, tiles, column, out, rows, ncol, offset=None):
    slots, samples, width = column.shape
    order = column_order(ncol)
    step = stride(rows, ncol, 1 if offset is None else 0)
    blank = jnp.zeros((samples, width), jnp.bfloat16)
    for first in range(0, slots, GROUP):
        lines = []
        for g in range(GROUP):
            where = column[first + g]
            picked = jnp.zeros_like(directions[0])
            for j, direction in enumerate(directions):
                picked = jnp.where(where == j, direction, picked)
            picked = picked.astype(jnp.bfloat16)
            line = [picked if h == g else blank for h in range(GROUP)]
            lines.append(jnp.concatenate(line, axis=1))
        sent = lax.dot_general(
            jnp.concatenate(lines, axis=0),
            tiles[first // GROUP],
            (((1,), (1,)), ((), ())),
            preferred_element_type=jnp.float32,
        )
        for g in range(GROUP):
            t = first + g
            mine = sent[g * samples : (g + 1) * samples].astype(jnp.bfloat16)
            for r in range(rows):
                place = step * (r * ncol + t % ncol) % (rows * ncol)
                if rows == 1:
                    place = order.index(t % ncol)
                if offset is None:
                    out[place, pl.ds((t // ncol) * samples, samples), :] = mine
                else:
                    pairs = samples // PAIR
                    begin = (t // ncol) * (pairs + 1)
                    out[place, pl.ds(begin, pairs)] = mine.reshape(pairs, PAIR, width)
                    out[place, begin + pairs] = (
                        offset[t][:PAIR].astype(jnp.float32).astype(jnp.bfloat16)
                    )


def part(packed, k, width):
    samples = packed.shape[0] - 1
    rhs = packed[:samples, k * width : (k + 1) * width]
    diag = packed[samples : samples + 1, k * width : (k + 1) * width]
    return rhs, diag


def coupled(moved, where, p, rows, ncol, share, samples, piece, kept=None):
    totals = [None] * piece
    pairs = samples // PAIR
    order = column_order(ncol)
    step = stride(rows, ncol, 1 if kept is None else 0)
    begin = step * (lax.axis_index("row") ^ p)
    for c in range(ncol):
        if moved.shape[0] == ncol:
            place = order.index(c)
        else:
            high, low = divmod(step * c % (rows * ncol), ncol)
            place = ((begin + high) & (rows - 1)) * ncol + low
        for a in range(share):
            keep = (p * ncol + c) * share + a
            if kept is not None:
                first = a * (pairs + 1)
                term = moved[place, pl.ds(first, pairs)].reshape(samples, moved.shape[3])
                off = moved[place, first + pairs].astype(jnp.float32)[:1]
                off = jnp.broadcast_to(off, term.shape)
                kept[keep] = off
            else:
                term = moved[place, pl.ds(a * samples, samples), :]
                off = where[keep]
            term = term.astype(jnp.float32)
            for k in range(piece):
                mine = jnp.where(off == k, term, 0.0)
                totals[k] = mine if totals[k] is None else totals[k] + mine
    return totals


def first_kernel(dims, *refs):
    rows, ncol, piece, width = dims
    packed = refs[:rows]
    tiles, column, offset, out = refs[rows:]
    directions = []
    for p in range(rows):
        for k in range(piece):
            rhs, diag = part(packed[p], k, width)
            directions.append((1.0 / theta) * (1.0 / diag) * rhs)
    multiply(directions, tiles, column, out, rows, ncol, offset)


def middle_kernel(dims, step, *refs):
    rows, ncol, piece, width = dims
    packed = refs[:rows]
    tiles, column, moved = refs[rows : rows + 3]
    samples = packed[0].shape[0] - 1
    share = column.shape[0] // ncol
    a, b = coefficients()[step]
    where = kept = None
    if step == 0:
        out, new_dir, new_res, new_sol, kept = refs[rows + 3 :]
    else:
        where, old_dir, old_res, old_sol, out, new_dir, new_res, new_sol = refs[rows + 3 :]
    directions = []
    for p in range(rows):
        image = coupled(moved, where, p, rows, ncol, share, samples, piece, kept)
        for k in range(piece):
            rhs, diag = part(packed[p], k, width)
            inverse = 1.0 / diag
            i = p * piece + k
            if step == 0:
                direction = (1.0 / theta) * inverse * rhs
                residual = rhs
                total = direction
            else:
                direction, residual, total = old_dir[i], old_res[i], old_sol[i]
            residual = residual - (diag * direction + image[k])
            direction = a * direction + b * inverse * residual
            if i < new_dir.shape[0]:
                new_dir[i] = direction
                new_res[i] = residual
                new_sol[i] = total + direction
            directions.append(direction)
    multiply(directions, tiles, column, out, out.shape[0] // ncol, ncol)


def last_kernel(dims, share, packed, where, moved, old_dir, old_res, old_sol, solution, residual):
    rows, ncol, piece, width = dims
    samples = packed.shape[0] - 1
    image = coupled(moved, where, 0, rows, ncol, share, samples, piece)
    for k in range(piece):
        lanes = slice(k * width, (k + 1) * width)
        diag = packed[samples : samples + 1, lanes]
        solution[:, lanes] = old_sol[k]
        residual[:, lanes] = old_res[k] - (diag * old_dir[k] + image[k])


def body(rhs, stiff_diag, tiles, tile_cols, tile_offsets, tile_counts):
    slots, width = tiles.shape[2:4]
    rows, ncol = lax.axis_size("row"), lax.axis_size("col")
    share = slots // ncol
    piece = stiff_diag.shape[0] // width
    samples = rhs.shape[0]
    blocks = rows * piece
    dims = (rows, ncol, piece, width)
    vmem = pl.BlockSpec(memory_space=pltpu.VMEM)
    hbm = pl.BlockSpec(memory_space=pltpu.HBM)
    state = jax.ShapeDtypeStruct((blocks, samples, width), jnp.float32)
    grouped = jax.ShapeDtypeStruct((slots // GROUP, width, GROUP * width), tiles.dtype)
    kept = jax.ShapeDtypeStruct((rows * ncol * share, samples, width), jnp.float32)
    own = jax.ShapeDtypeStruct((piece, samples, width), jnp.float32)
    table = jax.ShapeDtypeStruct((slots, samples, width), jnp.int32)
    narrow = jax.ShapeDtypeStruct((ncol, share * samples, width), jnp.bfloat16)
    message = jax.ShapeDtypeStruct((rows * ncol, share * samples, width), jnp.bfloat16)
    wide = jax.ShapeDtypeStruct(
        (rows * ncol, share * (samples // PAIR + 1), PAIR, width), jnp.bfloat16
    )
    params = pltpu.CompilerParams(vmem_limit_bytes=VMEM_BYTES)

    def exchange(x, turn):
        everyone = [0] * (rows * ncol)
        for i in range(rows * ncol):
            everyone[stride(rows, ncol, turn) * i % (rows * ncol)] = i
        return lax.all_to_all(
            x, ("row", "col"), 0, 0, axis_index_groups=[everyone], tiled=True
        )

    def exchange_columns(x):
        return lax.all_to_all(
            x, "col", 0, 0, axis_index_groups=[column_order(ncol)], tiled=True
        )

    def far(x):
        return pltpu.with_memory_space_constraint(x, pltpu.HBM)

    packed = pl.pallas_call(
        pack_kernel,
        out_shape=jax.ShapeDtypeStruct((samples + 1, rhs.shape[1]), jnp.float32),
        in_specs=[hbm] * 2,
        out_specs=vmem,
        scratch_shapes=[
            pltpu.VMEM((1, rhs.shape[1]), jnp.float32),
            pltpu.SemaphoreType.DMA((2,)),
        ],
        compiler_params=params,
    )(far(rhs), far(stiff_diag[None, :]))
    held, column, offset = pl.pallas_call(
        functools.partial(prep_kernel, piece),
        out_shape=(grouped, table, table),
        in_specs=[hbm] * 2 + [pl.BlockSpec(memory_space=pltpu.SMEM)] + [hbm],
        out_specs=(vmem,) * 3,
        scratch_shapes=[
            pltpu.SMEM(tile_cols.shape, jnp.int32),
            pltpu.SMEM(tile_offsets.shape, jnp.int32),
            pltpu.SemaphoreType.DMA((slots + 2,)),
        ],
        compiler_params=params,
        cost_estimate=pl.CostEstimate(flops=0, bytes_accessed=4 << 20, transcendentals=0),
    )(far(tile_cols), far(tile_offsets), tile_counts, far(tiles))

    pieces = {0: packed}
    for p in range(1, rows):
        pieces[p] = lax.ppermute(packed, "row", [(i, i ^ p) for i in range(rows)])
    pieces = [pieces[p] for p in range(rows)]
    sent = pl.pallas_call(
        functools.partial(first_kernel, dims),
        out_shape=wide,
        in_specs=[vmem] * (rows + 3),
        out_specs=vmem,
        compiler_params=params,
    )(*pieces, held, column, offset)
    moved = exchange(sent, 0)
    states = []
    for step in range(STEPS - 1):
        shapes = [message, state, state, state]
        if step + 2 == STEPS:
            shapes = [narrow, own, own, own]
        if step == 0:
            shapes.append(kept)
        results = pl.pallas_call(
            functools.partial(middle_kernel, dims, step),
            out_shape=shapes,
            in_specs=[vmem] * (rows + 3 + len(states)),
            out_specs=[vmem] * len(shapes),
            compiler_params=params,
        )(*pieces, held, column, moved, *states)
        sent = results[0]
        if step == 0:
            where = results[4]
        states = [where, *results[1:4]]
        moved = exchange(sent, 1) if step + 2 < STEPS else exchange_columns(sent)
    out = jax.ShapeDtypeStruct(rhs.shape, jnp.float32)
    return pl.pallas_call(
        functools.partial(last_kernel, dims, share),
        out_shape=(out, out),
        in_specs=[vmem] * 6,
        out_specs=(vmem, vmem),
        compiler_params=params,
    )(packed, where, moved, *states[1:])


def solution(mesh):
    in_specs = (
        P(None, ("row", "col")),
        P(("row", "col")),
        P("row", "col", None, None, None),
        P("row", "col", None),
        P("row", "col", None),
        P("row", "col", None),
    )
    out_specs = (P(None, ("row", "col")), P(None, ("row", "col")))
    return jax.shard_map(body, mesh=mesh, in_specs=in_specs, out_specs=out_specs, check_vma=False)
```
